256 devices in a mesh: batch: 64 (over y, z, core), feat: 4 (over x).
Axes of the slice: x: 4, y: 4, z: 8, core: 2. Of those that a mesh axis runs over, the one named last changes fastest.
Arguments:
- tables: bfloat16 [4, 128, 2048, 192], P('feat', 'batch'), may hold values from -3 to 3
- bag_ids: int32 [4, 128, 4, 8192], P('feat', 'batch'), may hold values from 0 to 2047
- bag_lengths: int32 [4, 128, 8192], P('feat', 'batch'), may hold values from 1 to 4
- pair_groups: int32 [16, 2], replicated, may hold values from 0 to 15
- compress: bfloat16 [16, 32, 8], P('feat'), may hold values from -1 to 1
- w_hidden: bfloat16 [16, 32, 8, 4096], P('feat'), may hold values from -0.09375 to 0.09375
- hidden_bias: float32 [4096], replicated, may hold values from -4 to 4
- norm_gain: float32 [4096], P('feat'), may hold values from 0.1 to 1.9
Outputs:
- interacted: bfloat16 [8192, 4096], P('batch', 'feat')
The draws below stay inside these ranges and needn't reach their ends.
Inputs may be any that keep to these rules, and one draw needn't show every extreme that they name: `bag_lengths`: ids at slots from a bag's length on are ignored.
All inputs are finite; a program needn't handle non-finite values.
Results may differ from the reference program's by a relative error of at most 0.0052.
Values may be sent and summed in bfloat16 or wider, within the bound.
A program may use at most 128 MiB of HBM per device.

```python
import jax
import jax.numpy as jnp
from jax import lax

F = 512
DIM = 192
HID = 4096
FG = 32
K = 8
ROWS = 2048
BAG = 4
B_DEV = 128
B_ALL = 8192
G = 16
NP = 16
FBLK = 4
FPB = 128
N_BATCH = 64


def touch_ends(drawn, key, low, high):
    place = [jax.random.randint(jax.random.fold_in(key, axis), (), 0, length) for axis, length in enumerate(drawn.shape)]
    widest = drawn.shape.index(max(drawn.shape))
    beside = place[:widest] + [(place[widest] + 1) % drawn.shape[widest]] + place[widest + 1:]
    return drawn.at[tuple(place)].set(low).at[tuple(beside)].set(high)


def block_levels(stream_key, dims, cuts, least, largest):
    gain, own = 1.0, jax.random.fold_in(stream_key, 6)
    for axis_at, blocks in cuts:
        steps = jnp.exp(jax.random.uniform(jax.random.fold_in(own, axis_at), (blocks,), jnp.float32, least / len(cuts), largest / len(cuts)))
        gain = gain * jnp.repeat(steps, dims[axis_at] // blocks).reshape([-1 if axis == axis_at else 1 for axis in range(len(dims))])
    return gain


def bell_draw(key, shape, scale, most, shards=(), kind=jnp.bfloat16):
    gain = block_levels(key, shape, shards, -0.22, 0.18) if shards else 1.0
    values = jax.random.normal(key, shape, jnp.float32) * scale * gain
    return jnp.minimum(jnp.maximum(values, -most), most).astype(kind)


def setup_inputs(seed: int = 0) -> dict:
    splits = jax.random.split(jax.random.key(seed), 9)
    return {
        "tables": bell_draw(splits[0], (FBLK, FPB, ROWS, DIM), 0.5, 3.0, ((0, 4), (1, 64))),
        "bag_ids": touch_ends(jax.random.randint(splits[1], (FBLK, FPB, BAG, B_ALL), 0, ROWS), jax.random.fold_in(splits[1], 1), 0, ROWS - 1).astype(jnp.int32),
        "bag_lengths": touch_ends(jax.random.randint(splits[2], (FBLK, FPB, B_ALL), 1, BAG + 1), jax.random.fold_in(splits[2], 1), 1, BAG).astype(jnp.int32),
        "pair_groups": touch_ends(jax.random.randint(splits[3], (NP, 2), 0, G), jax.random.fold_in(splits[3], 1), 0, G - 1).astype(jnp.int32),
        "compress": bell_draw(splits[4], (NP, FG, K), FG ** -0.5, 1.0, ((0, 4),)),
        "w_hidden": bell_draw(splits[5], (NP, FG, K, HID), (NP * FG * K) ** -0.5, 0.09375, ((0, 4),)),
        "hidden_bias": bell_draw(splits[6], (HID,), 1.0, 4.0, (), jnp.float32),
        "norm_gain": jnp.clip(1.0 + 0.18 * jax.random.normal(splits[7], (HID,), jnp.float32), 0.1, 1.9),
    }


def reference(tables, bag_ids, bag_lengths, pair_groups, compress, w_hidden, hidden_bias, norm_gain):
    flat_tables = tables.reshape(F, ROWS, DIM)
    flat_ids = bag_ids.reshape(F, BAG, B_ALL)
    flat_lengths = bag_lengths.reshape(F, B_ALL)
    w_flat = w_hidden.reshape(NP * FG * K, HID)
    compress_wide = compress.astype(jnp.float32)
    feature_index = jnp.arange(F, dtype=jnp.int32)
    bag_slots = jnp.arange(BAG, dtype=jnp.int32)
    gram_scale = float(DIM) ** (-0.5)

    def one_block(block_index):
        row_start = (block_index * B_DEV).astype(jnp.int32)
        block_ids = lax.dynamic_slice_in_dim(flat_ids, row_start, B_DEV, 2)
        block_lengths = lax.dynamic_slice_in_dim(flat_lengths, row_start, B_DEV, 1)
        picked = flat_tables[feature_index[:, None, None], block_ids].astype(jnp.float32)
        live_mask = (bag_slots[None, None, :] < block_lengths[:, :, None]).astype(jnp.float32)
        pooled = jnp.einsum('fbk,fkbd->fbd', live_mask, picked).astype(jnp.bfloat16)
        grouped = pooled.reshape(G, FG, B_DEV, DIM)
        row_blocks = grouped[pair_groups[:, 0]].astype(jnp.float32)
        col_blocks = grouped[pair_groups[:, 1]].astype(jnp.float32)
        gram_blocks = jnp.einsum('qfbd,qgbd->qbfg', row_blocks, col_blocks) * gram_scale
        squeezed = jnp.einsum('qbfg,qgk->bqfk', gram_blocks, compress_wide).astype(jnp.bfloat16)
        hidden = jnp.dot(squeezed.reshape(B_DEV, NP * FG * K), w_flat, preferred_element_type=jnp.float32)
        hidden = hidden + hidden_bias.astype(jnp.float32)[None, :]
        row_mean = lax.optimization_barrier(jnp.mean(hidden, axis=1, keepdims=True))
        spread = lax.optimization_barrier(jnp.mean(hidden * hidden, axis=1, keepdims=True)) - row_mean * row_mean
        normed = (hidden - row_mean) * lax.rsqrt(spread + 1e-05) * norm_gain.astype(jnp.float32)[None, :]
        return jax.nn.silu(normed).astype(jnp.bfloat16)
    all_blocks = lax.map(one_block, jnp.arange(N_BATCH, dtype=jnp.int32))
    return all_blocks.reshape(B_ALL, HID)
```

```python
import jax
import jax.numpy as jnp
from jax import lax
from jax.experimental import pallas as pl
from jax.experimental.pallas import tpu as pltpu
from jax.sharding import PartitionSpec as P

MESH = pl.DeviceIdType.MESH
BF = jnp.bfloat16
F32 = jnp.float32
NY, NZ, NX = 4, 8, 4
SRC = 256
SD = 32
DIM = 192
ROWS = 2048
LANES = 2 * DIM
CH = 256
NCH = 32
LAG = 8


def kernel(tt, ids, lens, pick, cpart, w_hbm, bias, gain, out,
           oh, send, recv, rf, cexp, expand, sqf, sq, lhs, w, part, partin, own, stats, statin,
           ssem, rsem, lsem, csem_s, csem_r, qsem_s, qsem_r, psem_s, psem_r, tsem_s, tsem_r, wsem):
    b = lax.axis_index("batch")
    x = lax.axis_index("feat")
    y = b // 16
    z = lax.rem(b // 2, NZ)
    c = lax.rem(b, 2)
    me = x * 64 + b

    bar = pltpu.get_barrier_semaphore()

    @pl.loop(1, 256)
    def _(i):
        tx = lax.rem(x + i // 64, NX)
        r = lax.rem(i, 64)
        ty = lax.rem(y + r // 16, NY)
        tz = lax.rem(z + lax.rem(r // 2, NZ), NZ)
        tc = lax.rem(c + lax.rem(r, 2), 2)
        pl.semaphore_signal(bar, inc=1, device_id=((ty * NZ + tz) * 2 + tc, tx), device_id_type=MESH)

    wcopy = pltpu.make_async_copy(w_hbm, w, wsem)
    wcopy.start()

    row = lax.broadcasted_iota(jnp.int32, (256, 256), 0)
    col = lax.broadcasted_iota(jnp.int32, (256, 256), 1)
    expand[...] = ((row // 128 == lax.rem(col // 8, 2)) & (lax.rem(row, 8) == lax.rem(col, 8))).astype(F32).astype(BF)

    def where_to(t):
        cy = lax.rem(y + t // 8, NY)
        cz = lax.rem(z + lax.rem(3 * lax.rem(t, 8) + 4, 8), NZ)
        return cy * NZ + cz

    def pool(t):
        chip = where_to(t)
        at = pl.multiple_of(chip * CH, CH)
        sums = []
        for e in range(2):
            length = lens[pl.ds(e, 1), pl.ds(at, CH)]
            live = [jnp.where(length > k, ids[e, pl.ds(k, 1), pl.ds(at, CH)], -4096 - k) for k in range(4)]
            keyed, counts = [], []
            for k in range(4):
                count = jnp.ones((1, CH), F32)
                for m in range(k + 1, 4):
                    count = count + jnp.where(live[m] == live[k], 1.0, 0.0)
                key = live[k]
                for m in range(k):
                    key = jnp.where(live[m] == live[k], -4096, key)
                keyed.append(key)
                counts.append(count.astype(BF))
            base = lax.broadcasted_iota(jnp.int32, (256, CH), 0).astype(F32).astype(BF)
            for j in range(8):
                hot = jnp.zeros((256, CH), BF)
                for k in range(3, -1, -1):
                    key = (keyed[k] - 256 * j).astype(F32).astype(BF)
                    hot = jnp.where(base == key, counts[k], hot)
                oh[e, pl.ds(j * 256, 256), :] = hot
            sums.append(jnp.dot(tt[e], oh[e], preferred_element_type=F32))
        full = jnp.concatenate([sums[0], sums[1][128:], sums[1][:128]], axis=0)
        send[chip] = full.T.astype(BF).reshape(2, NX, SD, LANES)

    def send_one(t, dx, dc):
        chip = where_to(t)
        tx = lax.rem(x + dx, NX)
        tc = lax.rem(c + dc, 2)
        pltpu.make_async_remote_copy(
            src_ref=send.at[chip, tc, tx], dst_ref=recv.at[me], send_sem=ssem, recv_sem=rsem,
            device_id=(chip * 2 + tc, tx), device_id_type=MESH).start()

    def send_chunk(t):
        for dx in range(NX):
            for dc in range(2):
                if dx == 0 and dc == 0:
                    @pl.when(t != 4)
                    def _():
                        send_one(t, dx, dc)
                else:
                    send_one(t, dx, dc)

    def c_copy(dx):
        tx = lax.rem(x + dx, NX)
        return pltpu.make_async_remote_copy(
            src_ref=cpart, dst_ref=cexp.at[x], send_sem=csem_s.at[dx], recv_sem=csem_r.at[dx],
            device_id=(b, tx), device_id_type=MESH)

    @pl.loop(0, NCH)
    def _(t):
        pool(t)

        @pl.when(t == LAG)
        def _():
            pl.semaphore_wait(bar, 255)
            for dx in range(1, NX):
                c_copy(dx).start()

            @pl.loop(0, LAG - 1)
            def _(u):
                send_chunk(u)

        @pl.when(t >= LAG)
        def _():
            send_chunk(t - 1)

    send_chunk(NCH - 1)
    mine = pltpu.make_async_copy(send.at[y * NZ + z, c, x], recv.at[me], lsem)
    mine.start()
    cexp[x] = cpart[...]
    for dx in range(1, NX):
        c_copy(dx).wait()
    mine.wait()
    every = pltpu.make_async_remote_copy(
        src_ref=recv.at[pl.ds(0, SRC - 1)], dst_ref=recv.at[pl.ds(0, SRC - 1)], send_sem=ssem, recv_sem=rsem,
        device_id=(b, lax.rem(x + 1, NX)), device_id_type=MESH)
    every.wait()

    @pl.loop(0, SRC // 8)
    def _(i):
        block = recv[pl.ds(i * 8, 8)].reshape(8 * SD, LANES).astype(F32)
        for q in range(3):
            rf[q, pl.ds(pl.multiple_of(i * 8 * SD, 8 * SD), 8 * SD), :] = block[:, q * 128:(q + 1) * 128]

    lane = lax.broadcasted_iota(jnp.int32, (128, 128), 1)
    pr = lax.broadcasted_iota(jnp.int32, (256, 256), 0)
    pc = lax.broadcasted_iota(jnp.int32, (256, 256), 1)
    scale = float(DIM) ** -0.5
    low = lane < 64

    @pl.loop(0, SD)
    def _(s):
        one = jnp.concatenate([rf[q, pl.ds(s, SRC, stride=SD), :] for q in range(3)], 1).astype(BF)
        u0 = jnp.dot(cexp[:, 0].reshape(128, 256), one[:, :256], preferred_element_type=F32)
        u1 = jnp.dot(cexp[:, 1].reshape(128, 256), one[:, 128:], preferred_element_type=F32)
        va = u0[:, :128] + u1[:, 128:]
        vb = jnp.where(low, u0[:, 128:], u1[:, :128])
        vb = vb + pltpu.roll(vb, 64, 1)
        vb0 = jnp.where(low, vb, 0.0)
        vb1 = jnp.where(low, 0.0, vb)

        def two(v):
            hi = v.astype(BF)
            return hi, (v - hi.astype(F32)).astype(BF)
        ah, al = two(va)
        b0h, b0l = two(vb0)
        b1h, b1l = two(vb1)
        w0 = jnp.concatenate([jnp.concatenate([ah, b0h], 1), jnp.concatenate([al, b0l], 1)], 0)
        w1 = jnp.concatenate([jnp.concatenate([b1h, ah], 1), jnp.concatenate([b1l, al], 1)], 0)
        rows = jnp.dot(pick[...], one, preferred_element_type=F32).astype(BF)
        dims = (((1,), (1,)), ((), ()))
        s0 = lax.dot_general(rows[:, :256], w0, dims, preferred_element_type=F32)
        s1 = lax.dot_general(rows[:, 128:], w1, dims, preferred_element_type=F32)
        both = jnp.concatenate([s0[:, :128] + s0[:, 128:], s1[:, :128] + s1[:, 128:]], 1) * scale
        both = jnp.where(pr // 16 == lax.rem(pc // 8, 16), both, 0.0).astype(BF)
        wide = jnp.dot(both, expand[...], preferred_element_type=F32)
        wide = jnp.where(lax.rem(pr, 16) == pc // 16, wide, 0.0)
        line = jnp.sum(wide.reshape(16, 16, 256), axis=1)
        for q in range(2):
            sqf[q, pl.ds(s, 16, stride=SD), :] = line[:, q * 128:(q + 1) * 128]

    for q in range(2):
        sq[:, :, :, q * 128:(q + 1) * 128] = sqf[q].astype(BF).reshape(4, 4, SD, 128)

    def q_copy(dx):
        tx = lax.rem(x + dx, NX)
        return pltpu.make_async_remote_copy(
            src_ref=sq.at[tx], dst_ref=lhs.at[x], send_sem=qsem_s.at[dx], recv_sem=qsem_r.at[dx],
            device_id=(b, tx), device_id_type=MESH)

    for dx in range(1, NX):
        q_copy(dx).start()
    lhs[x] = sq[x]
    wcopy.wait()
    for dx in range(1, NX):
        q_copy(dx).wait()

    def p_copy(dx):
        tx = lax.rem(x + dx, NX)
        return pltpu.make_async_remote_copy(
            src_ref=part.at[dx - 1], dst_ref=partin.at[dx - 1], send_sem=psem_s.at[dx - 1], recv_sem=psem_r.at[dx - 1],
            device_id=(b, tx), device_id_type=MESH)

    for dx in (2, 1, 3, 0):
        tx = lax.rem(x + dx, NX)

        @pl.loop(0, 4)
        def _(n):
            cols = pl.ds(pl.multiple_of(tx * 1024 + n * 256, 256), 256)
            acc = jnp.zeros((128, 256), F32)
            for p in range(4):
                acc = acc + jnp.dot(lhs[:, p].reshape(128, 256), w[p, :, cols], preferred_element_type=F32)
            here = pl.ds(pl.multiple_of(n * 256, 256), 256)
            if dx == 0:
                own[:, here] = acc + bias[:, cols]
            else:
                part[dx - 1, :, here] = acc.astype(BF)
        if dx != 0:
            p_copy(dx).start()
    for dx in range(1, NX):
        p_copy(dx).wait()
    hidden = own[...]
    for dx in range(1, NX):
        hidden = hidden + partin[dx - 1].astype(F32)
    own[...] = hidden
    rsum = jnp.sum(hidden, axis=1, keepdims=True)
    rsq = jnp.sum(hidden * hidden, axis=1, keepdims=True)
    both = jnp.where(lane == 0, rsum, jnp.where(lane == 1, rsq, 0.0))
    stats[...] = both.T[:8]

    def t_copy(dx):
        tx = lax.rem(x + dx, NX)
        return pltpu.make_async_remote_copy(
            src_ref=stats, dst_ref=statin.at[dx - 1], send_sem=tsem_s.at[dx - 1], recv_sem=tsem_r.at[dx - 1],
            device_id=(b, tx), device_id_type=MESH)

    for dx in range(1, NX):
        t_copy(dx).start()
    for dx in range(1, NX):
        t_copy(dx).wait()
    total = (stats[...] + statin[0] + statin[1] + statin[2]) * (1.0 / 4096.0)
    mean = total[0:1]
    inv = lax.rsqrt(total[1:2] - mean * mean + 1e-05)
    back = jnp.concatenate([mean, inv, jnp.zeros((126, 128), F32)], 0).T
    v = (own[...] - back[:, 0:1]) * back[:, 1:2] * gain[...]
    out[...] = (v / (1.0 + jnp.exp(-v))).astype(BF)


def body(tables, bag_ids, bag_lengths, pair_groups, compress, w_hidden, hidden_bias, norm_gain):
    x = lax.axis_index("feat")
    local = lax.dynamic_slice_in_dim(pair_groups, x * 4, 4, 0)
    comp = compress.reshape(4, 16, 2, 8).transpose(2, 0, 3, 1)
    hit = (jnp.arange(16, dtype=jnp.int32)[None, :] == local[:, 1:2])[None, :, None, :, None]
    cpart = jnp.where(hit, comp[:, :, :, None, :], jnp.zeros((), BF)).reshape(2, 32, 256)
    slots = jnp.arange(256, dtype=jnp.int32)
    want = jnp.repeat(pair_groups[:, 0], 16) * 16 + slots % 16
    pick = (want[:, None] == slots[None, :]).astype(BF)
    vm = pl.BlockSpec(memory_space=pltpu.VMEM)
    sem = pltpu.SemaphoreType.DMA
    return pl.pallas_call(
        kernel,
        out_shape=jax.ShapeDtypeStruct((128, 1024), BF),
        in_specs=[vm, vm, vm, vm, vm, pl.BlockSpec(memory_space=pl.ANY), vm, vm],
        out_specs=vm,
        scratch_shapes=[
            pltpu.VMEM((2, ROWS, CH), BF),
            pltpu.VMEM((NCH, 2, NX, SD, LANES), BF),
            pltpu.VMEM((SRC, SD, LANES), BF),
            pltpu.VMEM((3, SRC * SD, 128), F32),
            pltpu.VMEM((4, 2, 32, 256), BF),
            pltpu.VMEM((256, 256), BF),
            pltpu.VMEM((2, 16 * SD, 128), F32),
            pltpu.VMEM((4, 4, SD, 256), BF),
            pltpu.VMEM((4, 4, SD, 256), BF),
            pltpu.VMEM((4, 256, 4096), BF),
            pltpu.VMEM((3, 128, 1024), BF),
            pltpu.VMEM((3, 128, 1024), BF),
            pltpu.VMEM((128, 1024), F32),
            pltpu.VMEM((8, 128), F32),
            pltpu.VMEM((3, 8, 128), F32),
            sem, sem, sem, sem((4,)), sem((4,)), sem((4,)), sem((4,)), sem((3,)), sem((3,)), sem((3,)), sem((3,)), sem,
        ],
        compiler_params=pltpu.CompilerParams(
            collective_id=0, has_side_effects=True, vmem_limit_bytes=60 << 20),
    )(tables[0].swapaxes(1, 2), bag_ids[0], bag_lengths[0], pick, cpart,
      w_hidden.reshape(4, 256, 4096), hidden_bias.reshape(1, 4096), norm_gain.reshape(1, 1024))


def solution(mesh):
    in_specs = (
        P("feat", "batch", None, None),
        P("feat", "batch", None, None),
        P("feat", "batch", None),
        P(),
        P("feat", None, None),
        P("feat", None, None, None),
        P(),
        P("feat"),
    )
    out_specs = P("batch", "feat")
    return jax.shard_map(body, mesh=mesh, in_specs=in_specs, out_specs=out_specs, check_vma=False)
```

```python
import jax
import jax.numpy as jnp
from jax import lax
from jax.experimental import pallas as pl
from jax.experimental.pallas import tpu as pltpu
from jax.sharding import PartitionSpec as P

MESH = pl.DeviceIdType.MESH
BF = jnp.bfloat16
F32 = jnp.float32
NY, NZ, NX = 4, 8, 4
SRC = 256
SD = 32
DIM = 192
ROWS = 2048
LANES = 2 * DIM
CH = 256
NR = 4
SPR = SD // NR
WID = 4 * SPR
UNITS = 32
UPR = UNITS // NR
LAG = 3


def kernel(tt, ids, lens, cpart, gmask, w_hbm, bias, gain, out,
           oh, send, recv, rf, cexp, perm, cs, cf, sq, lhs, w, part, partin, own, stats, statin,
           ssem, rsem, lsem, csem_s, csem_r, qsem_s, qsem_r, psem_s, psem_r, tsem_s, tsem_r, wsem):
    b = lax.axis_index("batch")
    x = lax.axis_index("feat")
    y = b // 16
    z = lax.rem(b // 2, NZ)
    c = lax.rem(b, 2)
    me = x * 64 + b

    bar = pltpu.get_barrier_semaphore()

    @pl.loop(0, 128)
    def _(i):
        tx = lax.rem(x + i // 32, NX)
        ty = lax.rem(y + lax.rem(i // 8, NY), NY)
        tz = lax.rem(z + lax.rem(i, NZ), NZ)
        at = (ty * NZ + tz) * 2
        pl.semaphore_signal(bar, inc=1, device_id=(at + 1 - c, tx), device_id_type=MESH)

        @pl.when(i != 0)
        def _():
            pl.semaphore_signal(bar, inc=1, device_id=(at + c, tx), device_id_type=MESH)

    @pl.loop(0, 16)
    def _(j):
        for p in range(4):
            pltpu.make_async_copy(
                w_hbm.at[p, pl.ds(pl.multiple_of(j * 16, 16), 16)],
                w.at[j // 4, pl.ds(pl.multiple_of(lax.rem(j, 4) * 64 + p * 16, 16), 16)], wsem).start()

    row = lax.broadcasted_iota(jnp.int32, (256, 256), 0)
    col = lax.broadcasted_iota(jnp.int32, (256, 256), 1)
    perm[...] = (col == lax.rem(row // 8, 16) * 16 + row // 128 * 8 + lax.rem(row, 8)).astype(F32).astype(BF)
    quarter = lax.broadcasted_iota(jnp.int32, (1, 128), 1) // WID

    def where_to(u, q):
        t = u * NR + q
        cy = lax.rem(y + t // 8, NY)
        cz = lax.rem(z + lax.rem(3 * lax.rem(t, 8) + 4, 8), NZ)
        return cy * NZ + cz

    def pool(r, u):
        chips = [where_to(u, q) for q in range(NR)]

        def lanes_of(ref):
            tiles = []
            for h in range(2):
                made = None
                for m in range(NR):
                    k = h * NR + m
                    at = pl.multiple_of((chips[k // 2] * 2 + k % 2) * 128, 128)
                    piece = pltpu.roll(ref[:, pl.ds(at, 128)], lax.rem(m * WID - r * WID + 128, 128), 1)
                    made = piece if m == 0 else jnp.where(quarter == m, piece, made)
                tiles.append(made)
            return jnp.concatenate(tiles, axis=1)

        both_lengths = lanes_of(lens)
        sums = []
        for e in range(2):
            length = both_lengths[e:e + 1]
            four = lanes_of(ids.at[e])
            live = [jnp.where(length > k, four[k:k + 1], -4096 - k) for k in range(4)]
            keyed, counts = [], []
            for k in range(4):
                count = jnp.ones((1, CH), F32)
                for m in range(k + 1, 4):
                    count = count + jnp.where(live[m] == live[k], 1.0, 0.0)
                key = live[k]
                for m in range(k):
                    key = jnp.where(live[m] == live[k], -4096, key)
                keyed.append(key)
                counts.append(count.astype(BF))
            base = lax.broadcasted_iota(jnp.int32, (256, CH), 0).astype(F32).astype(BF)
            for j in range(8):
                hot = jnp.zeros((256, CH), BF)
                for k in range(3, -1, -1):
                    key = (keyed[k] - 256 * j).astype(F32).astype(BF)
                    hot = jnp.where(base == key, counts[k], hot)
                oh[e, pl.ds(j * 256, 256), :] = hot
            sums.append(jnp.dot(tt[e], oh[e], preferred_element_type=F32))
        full = jnp.concatenate([sums[0], sums[1][128:], sums[1][:128]], axis=0)
        made = full.T.reshape(NR, 2, NX, SPR, LANES).astype(BF)
        for q in range(NR):
            send[r, chips[q]] = made[q]

    def send_one(r, u, q, dx, dc):
        chip = where_to(u, q)
        tx = lax.rem(x + dx, NX)
        tc = lax.rem(c + dc, 2)
        pltpu.make_async_remote_copy(
            src_ref=send.at[r, chip, tc, tx], dst_ref=recv.at[r, me], send_sem=ssem, recv_sem=rsem.at[r],
            device_id=(chip * 2 + tc, tx), device_id_type=MESH).start()

    def send_unit(t):
        r = t // UPR
        u = lax.rem(t, UPR)
        for dx in range(NX):
            for dc in range(2):
                for q in range(NR):
                    if dx == 0 and dc == 0 and q == 4 % NR:
                        @pl.when(u != 4 // NR)
                        def _():
                            send_one(r, u, q, dx, dc)
                    else:
                        send_one(r, u, q, dx, dc)

    def c_copy(dx):
        tx = lax.rem(x + dx, NX)
        return pltpu.make_async_remote_copy(
            src_ref=cpart, dst_ref=cexp.at[x], send_sem=csem_s.at[dx], recv_sem=csem_r.at[dx],
            device_id=(b, tx), device_id_type=MESH)

    @pl.loop(0, UNITS)
    def _(t):
        pool(t // UPR, lax.rem(t, UPR))

        @pl.when(t == LAG)
        def _():
            pl.semaphore_wait(bar, 255)
            for dx in range(1, NX):
                c_copy(dx).start()

            @pl.loop(0, LAG - 1)
            def _(u):
                send_unit(u)

        @pl.when(t >= LAG)
        def _():
            send_unit(t - 1)

    send_unit(UNITS - 1)

    def mine(r):
        return pltpu.make_async_copy(send.at[r, y * NZ + z, c, x], recv.at[r, me], lsem.at[r])

    for r in range(NR):
        mine(r).start()
    cexp[x] = cpart[...]
    for dx in range(1, NX):
        c_copy(dx).wait()
    pltpu.make_async_copy(w_hbm, w, wsem).wait()

    lane = lax.broadcasted_iota(jnp.int32, (128, 128), 1)
    scale = float(DIM) ** -0.5
    low = lane < 64

    def gram(s):
        one = jnp.concatenate([rf[q, pl.ds(s, SRC, stride=SPR), :] for q in range(3)], 1).astype(BF)
        u0 = jnp.dot(cexp[:, 0].reshape(128, 256), one[:, :256], preferred_element_type=F32)
        u1 = jnp.dot(cexp[:, 1].reshape(128, 256), one[:, 128:], preferred_element_type=F32)
        va = u0[:, :128] + u1[:, 128:]
        vb = jnp.where(low, u0[:, 128:], u1[:, :128])
        vb = vb + pltpu.roll(vb, 64, 1)
        vb0 = jnp.where(low, vb, 0.0)
        vb1 = jnp.where(low, 0.0, vb)

        def two(v):
            hi = v.astype(BF)
            return hi, (v - hi.astype(F32)).astype(BF)
        ah, al = two(va)
        b0h, b0l = two(vb0)
        b1h, b1l = two(vb1)
        w0 = jnp.concatenate([jnp.concatenate([ah, b0h], 1), jnp.concatenate([al, b0l], 1)], 0)
        w1 = jnp.concatenate([jnp.concatenate([b1h, ah], 1), jnp.concatenate([b1l, al], 1)], 0)
        dims = (((1,), (1,)), ((), ()))
        lines = []
        for e, (rows, ww) in enumerate(((one[:, :256], w0), (one[:, 128:], w1))):
            se = lax.dot_general(rows, ww, dims, preferred_element_type=F32)
            se = (se[:, :128] + se[:, 128:]).reshape(16, 16, 128)
            got = jnp.where(gmask[0:1, :] > 0.5, se[0], 0.0)
            for g in range(1, 16):
                got = jnp.where(gmask[g:g + 1, :] > 0.5, se[g], got)
            lines.append(got * scale)
        return jnp.concatenate(lines, 1).astype(BF)

    def q_copy(r, dx):
        tx = lax.rem(x + dx, NX)
        return pltpu.make_async_remote_copy(
            src_ref=sq.at[r, tx], dst_ref=lhs.at[r, x], send_sem=qsem_s.at[r, dx], recv_sem=qsem_r.at[r, dx],
            device_id=(b, tx), device_id_type=MESH)

    def p_copy(r, dx):
        tx = lax.rem(x + dx, NX)
        return pltpu.make_async_remote_copy(
            src_ref=part.at[r, dx - 1], dst_ref=partin.at[r, dx - 1],
            send_sem=psem_s.at[r, dx - 1], recv_sem=psem_r.at[r, dx - 1],
            device_id=(b, tx), device_id_type=MESH)

    def t_copy(r, dx):
        tx = lax.rem(x + dx, NX)
        return pltpu.make_async_remote_copy(
            src_ref=stats.at[r], dst_ref=statin.at[r, dx - 1],
            send_sem=tsem_s.at[r, dx - 1], recv_sem=tsem_r.at[r, dx - 1],
            device_id=(b, tx), device_id_type=MESH)

    @pl.loop(0, NR)
    def _(r):
        mine(r).wait()
        pltpu.make_async_remote_copy(
            src_ref=recv.at[r, pl.ds(0, SRC - 1)], dst_ref=recv.at[r, pl.ds(0, SRC - 1)],
            send_sem=ssem, recv_sem=rsem.at[r],
            device_id=(b, lax.rem(x + 1, NX)), device_id_type=MESH).wait_recv()

        @pl.loop(0, SRC // 16)
        def _(i):
            block = recv[r, pl.ds(i * 16, 16)].astype(F32).reshape(16 * SPR, LANES)
            for q in range(3):
                rf[q, pl.ds(pl.multiple_of(i * 16 * SPR, 16 * SPR), 16 * SPR), :] = block[:, q * 128:(q + 1) * 128]

        @pl.loop(0, SPR // 2)
        def _(h):
            first = gram(2 * h)
            second = gram(2 * h + 1)
            cs[pl.ds(pl.multiple_of(h * 32, 32), 32), :] = jnp.concatenate([first, second], 0)

        turned = jnp.dot(cs[...], perm[...], preferred_element_type=F32)
        cf[0] = turned[:, :128]
        cf[1] = turned[:, 128:]
        for h in range(2):
            by_row = [cf[h, pl.ds(j, SPR, stride=16), :] for j in range(16)]
            for half in range(2):
                cut = [v[:, half * 64:half * 64 + 64] for v in by_row]
                for jj in range(4):
                    sq[r, h * 2 + half, jj] = jnp.concatenate(cut[4 * jj:4 * jj + 4], 1).astype(BF)

        for dx in range(1, NX):
            q_copy(r, dx).start()
        lhs[r, x] = sq[r, x]
        for dx in range(1, NX):
            q_copy(r, dx).wait()

        for dx in (2, 1, 3, 0):
            tx = lax.rem(x + dx, NX)

            @pl.loop(0, 4)
            def _(n):
                cols = pl.ds(pl.multiple_of(tx * 1024 + n * 256, 256), 256)
                acc = jnp.zeros((WID, 256), F32)
                for jj in range(4):
                    acc = acc + jnp.dot(lhs[r, :, jj].reshape(WID, 256), w[jj, :, cols], preferred_element_type=F32)
                here = pl.ds(pl.multiple_of(n * 256, 256), 256)
                if dx == 0:
                    own[:, here] = acc + bias[:, cols]
                else:
                    part[r, dx - 1, :, here] = acc.astype(BF)
            if dx != 0:
                p_copy(r, dx).start()
        for dx in range(1, NX):
            p_copy(r, dx).wait()
        hidden = own[...]
        for dx in range(1, NX):
            hidden = hidden + partin[r, dx - 1].astype(F32)
        own[...] = hidden
        rsum = jnp.sum(hidden, axis=1, keepdims=True)
        rsq = jnp.sum(hidden * hidden, axis=1, keepdims=True)
        at = lane[:WID]
        both = jnp.where(at == 0, rsum, jnp.where(at == 1, rsq, 0.0))
        stats[r] = jnp.concatenate([both, jnp.zeros((128 - WID, 128), F32)], 0).T[:8]
        for dx in range(1, NX):
            t_copy(r, dx).start()
        for dx in range(1, NX):
            t_copy(r, dx).wait()
        total = (stats[r] + statin[r, 0] + statin[r, 1] + statin[r, 2]) * (1.0 / 4096.0)
        mean = total[0:1]
        inv = lax.rsqrt(total[1:2] - mean * mean + 1e-05)
        back = jnp.concatenate([mean, inv, jnp.zeros((126, 128), F32)], 0).T[:WID]
        v = (own[...] - back[:, 0:1]) * back[:, 1:2] * gain[...]
        out[pl.ds(pl.multiple_of(r * WID, WID), WID), :] = (v / (1.0 + jnp.exp(-v))).astype(BF)

    sent = recv.at[:, pl.ds(0, SRC - 1)]
    pltpu.make_async_remote_copy(
        src_ref=sent, dst_ref=sent, send_sem=ssem, recv_sem=rsem.at[0],
        device_id=(b, lax.rem(x + 1, NX)), device_id_type=MESH).wait_send()


def body(tables, bag_ids, bag_lengths, pair_groups, compress, w_hidden, hidden_bias, norm_gain):
    x = lax.axis_index("feat")
    local = lax.dynamic_slice_in_dim(pair_groups, x * 4, 4, 0)
    comp = compress.reshape(4, 16, 2, 8).transpose(2, 0, 3, 1)
    groups = jnp.arange(16, dtype=jnp.int32)
    hit = (groups[None, :] == local[:, 1:2])[None, :, None, :, None]
    cpart = jnp.where(hit, comp[:, :, :, None, :], jnp.zeros((), BF)).reshape(2, 32, 256)
    gmask = (groups[:, None] == jnp.repeat(pair_groups[:, 0], 8)[None, :]).astype(F32)
    vm = pl.BlockSpec(memory_space=pltpu.VMEM)
    sem = pltpu.SemaphoreType.DMA
    return pl.pallas_call(
        kernel,
        out_shape=jax.ShapeDtypeStruct((128, 1024), BF),
        in_specs=[vm, vm, vm, vm, vm, pl.BlockSpec(memory_space=pl.ANY), vm, vm],
        out_specs=vm,
        scratch_shapes=[
            pltpu.VMEM((2, ROWS, CH), BF),
            pltpu.VMEM((NR, 32, 2, NX, SPR, LANES), BF),
            pltpu.VMEM((NR, SRC, SPR, LANES), BF),
            pltpu.VMEM((3, SRC * SPR, 128), F32),
            pltpu.VMEM((4, 2, 32, 256), BF),
            pltpu.VMEM((256, 256), BF),
            pltpu.VMEM((SPR * 16, 256), BF),
            pltpu.VMEM((2, SPR * 16, 128), F32),
            pltpu.VMEM((NR, 4, 4, SPR, 256), BF),
            pltpu.VMEM((NR, 4, 4, SPR, 256), BF),
            pltpu.VMEM((4, 256, 4096), BF),
            pltpu.VMEM((NR, 3, WID, 1024), BF),
            pltpu.VMEM((NR, 3, WID, 1024), BF),
            pltpu.VMEM((WID, 1024), F32),
            pltpu.VMEM((NR, 8, 128), F32),
            pltpu.VMEM((NR, 3, 8, 128), F32),
            sem, sem((NR,)), sem((NR,)), sem((4,)), sem((4,)), sem((NR, 4)), sem((NR, 4)),
            sem((NR, 3)), sem((NR, 3)), sem((NR, 3)), sem((NR, 3)), sem,
        ],
        compiler_params=pltpu.CompilerParams(
            collective_id=0, has_side_effects=True, vmem_limit_bytes=60 << 20),
    )(tables[0].swapaxes(1, 2), bag_ids[0], bag_lengths[0], cpart, gmask,
      w_hidden.reshape(4, 256, 4096), hidden_bias.reshape(1, 4096), norm_gain.reshape(1, 1024))


def solution(mesh):
    in_specs = (
        P("feat", "batch", None, None),
        P("feat", "batch", None, None),
        P("feat", "batch", None),
        P(),
        P("feat", None, None),
        P("feat", None, None, None),
        P(),
        P("feat"),
    )
    out_specs = P("batch", "feat")
    return jax.shard_map(body, mesh=mesh, in_specs=in_specs, out_specs=out_specs, check_vma=False)
```

```python
import jax
import jax.numpy as jnp
from jax import lax
from jax.experimental import pallas as pl
from jax.experimental.pallas import tpu as pltpu
from jax.sharding import PartitionSpec as P

MESH = pl.DeviceIdType.MESH
BF = jnp.bfloat16
F32 = jnp.float32
NY, NZ, NX = 4, 8, 4
SRC = 256
SD = 32
DIM = 192
ROWS = 2048
LANES = 2 * DIM
CH = 256
NR = 4
SPR = SD // NR
WID = 4 * SPR
UNITS = 32
UPR = UNITS // NR
LAG = 3


def kernel(tt, ids, lens, pairs, comp, w_hbm, bias, gain, out,
           oh, send, recv, rf, cpart, gmask, cexp, perm, cs, cf, sq, lhs, w, part, partin, own, stats, statin,
           ssem, rsem, lsem, csem_s, csem_r, qsem_s, qsem_r, psem_s, psem_r, tsem_s, tsem_r, wsem):
    b = lax.axis_index("batch")
    x = lax.axis_index("feat")
    y = b // 16
    z = lax.rem(b // 2, NZ)
    c = lax.rem(b, 2)
    me = x * 64 + b

    bar = pltpu.get_barrier_semaphore()

    along_z = [lax.rem(z + k, NZ) * 2 for k in range(NZ)]
    for dx in range(NX):
        tx = lax.rem(x + dx, NX)
        for dy in range(NY):
            plane = lax.rem(y + dy, NY) * (2 * NZ)
            for k in range(NZ):
                if dx + dy + k > 0:
                    pl.semaphore_signal(bar, inc=1, device_id=(plane + along_z[k] + c, tx), device_id_type=MESH)
                pl.semaphore_signal(bar, inc=1, device_id=(plane + along_z[k] + 1 - c, tx), device_id_type=MESH)

    @pl.loop(0, 16)
    def _(j):
        for p in range(4):
            pltpu.make_async_copy(
                w_hbm.at[p, pl.ds(pl.multiple_of(j * 16, 16), 16)],
                w.at[j // 4, pl.ds(pl.multiple_of(lax.rem(j, 4) * 64 + p * 16, 16), 16)], wsem).start()

    row = lax.broadcasted_iota(jnp.int32, (256, 256), 0)
    col = lax.broadcasted_iota(jnp.int32, (256, 256), 1)
    perm[...] = (col == lax.rem(row // 8, 16) * 16 + row // 128 * 8 + lax.rem(row, 8)).astype(F32).astype(BF)
    lane_pair = lax.broadcasted_iota(jnp.int32, (16, 128), 1) // 8
    first = jnp.zeros((16, 128), jnp.int32)
    for p in range(16):
        first = jnp.where(lane_pair == p, pairs[0, p], first)
    gmask[...] = (first == lax.broadcasted_iota(jnp.int32, (16, 128), 0)).astype(F32)
    row_pair = lax.broadcasted_iota(jnp.int32, (32, 256), 0) // 8
    second = jnp.zeros((32, 256), jnp.int32)
    for p in range(4):
        second = jnp.where(row_pair == p, pairs[1, x * 4 + p], second)
    hit = second == lax.broadcasted_iota(jnp.int32, (32, 256), 1) // 16
    slot = lax.broadcasted_iota(jnp.int32, (32, 256), 0)
    member = lax.rem(lax.broadcasted_iota(jnp.int32, (32, 256), 1), 16)
    for e in range(2):
        spread = (slot == 2 * member + e).astype(F32).astype(BF)
        cpart[e] = jnp.where(hit, jnp.dot(comp[...], spread, preferred_element_type=F32), 0.0).astype(BF)

    quarter = lax.broadcasted_iota(jnp.int32, (1, 128), 1) // WID

    def where_to(u, q):
        t = u * NR + q
        cy = lax.rem(y + q + t // 8, NY)
        cz = lax.rem(z + lax.rem(3 * lax.rem(t, 8) + 4, 8), NZ)
        return cy * NZ + cz

    def pool(r, u):
        chips = [where_to(u, q) for q in range(NR)]

        def lanes_of(ref):
            tiles = []
            for h in range(2):
                made = None
                for m in range(NR):
                    k = h * NR + m
                    at = pl.multiple_of((chips[k // 2] * 2 + k % 2) * 128, 128)
                    piece = pltpu.roll(ref[:, pl.ds(at, 128)], lax.rem(m * WID - r * WID + 128, 128), 1)
                    made = piece if m == 0 else jnp.where(quarter == m, piece, made)
                tiles.append(made)
            return jnp.concatenate(tiles, axis=1)

        both_lengths = lanes_of(lens)
        sums = []
        for e in range(2):
            length = both_lengths[e:e + 1]
            four = lanes_of(ids.at[e])
            live = [jnp.where(length > k, four[k:k + 1], -4096 - k) for k in range(4)]
            keyed, counts = [], []
            for k in range(4):
                count = jnp.ones((1, CH), F32)
                for m in range(k + 1, 4):
                    count = count + jnp.where(live[m] == live[k], 1.0, 0.0)
                key = live[k]
                for m in range(k):
                    key = jnp.where(live[m] == live[k], -4096, key)
                keyed.append(key)
                counts.append(count.astype(BF))
            base = lax.broadcasted_iota(jnp.int32, (256, CH), 0).astype(F32).astype(BF)
            for j in range(8):
                hot = jnp.zeros((256, CH), BF)
                for k in range(3, -1, -1):
                    key = (keyed[k] - 256 * j).astype(F32).astype(BF)
                    hot = jnp.where(base == key, counts[k], hot)
                oh[e, pl.ds(j * 256, 256), :] = hot
            sums.append(jnp.dot(tt[e], oh[e], preferred_element_type=F32))
        full = jnp.concatenate([sums[0], sums[1][128:], sums[1][:128]], axis=0)
        made = full.T.reshape(NR, 2, NX, SPR, LANES).astype(BF)
        for q in range(NR):
            send[r, chips[q]] = made[q]

    def send_one(r, u, q, dx, dc):
        chip = where_to(u, q)
        tx = lax.rem(x + dx, NX)
        tc = lax.rem(c + dc, 2)
        pltpu.make_async_remote_copy(
            src_ref=send.at[r, chip, tc, tx], dst_ref=recv.at[r, me], send_sem=ssem, recv_sem=rsem.at[r],
            device_id=(chip * 2 + tc, tx), device_id_type=MESH).start()

    def send_unit(t):
        r = t // UPR
        u = lax.rem(t, UPR)
        for shift in range(NX):
            for dc in range(2):
                for q in range(NR):
                    dx = (shift + q) % NX
                    if dx == 0 and dc == 0 and q == 4 % NR:
                        @pl.when(u != 4 // NR)
                        def _():
                            send_one(r, u, q, dx, dc)
                    else:
                        send_one(r, u, q, dx, dc)

    def c_copy(dx):
        tx = lax.rem(x + dx, NX)
        return pltpu.make_async_remote_copy(
            src_ref=cpart, dst_ref=cexp.at[x], send_sem=csem_s.at[dx], recv_sem=csem_r.at[dx],
            device_id=(b, tx), device_id_type=MESH)

    @pl.loop(0, UNITS)
    def _(t):
        pool(t // UPR, lax.rem(t, UPR))

        @pl.when(t == LAG)
        def _():
            pl.semaphore_wait(bar, 255)
            for dx in range(1, NX):
                c_copy(dx).start()

            @pl.loop(0, LAG - 1)
            def _(u):
                send_unit(u)

        @pl.when(t >= LAG)
        def _():
            send_unit(t - 1)

    send_unit(UNITS - 1)

    def mine(r):
        return pltpu.make_async_copy(send.at[r, y * NZ + z, c, x], recv.at[r, me], lsem.at[r])

    for r in range(NR):
        mine(r).start()
    cexp[x] = cpart[...]
    for dx in range(1, NX):
        c_copy(dx).wait()
    pltpu.make_async_copy(w_hbm, w, wsem).wait()

    lane = lax.broadcasted_iota(jnp.int32, (128, 128), 1)
    scale = float(DIM) ** -0.5
    low = lane < 64

    def gram(s):
        one = jnp.concatenate([rf[q, pl.ds(s, SRC, stride=SPR), :] for q in range(3)], 1).astype(BF)
        u0 = jnp.dot(cexp[:, 0].reshape(128, 256), one[:, :256], preferred_element_type=F32)
        u1 = jnp.dot(cexp[:, 1].reshape(128, 256), one[:, 128:], preferred_element_type=F32)
        va = u0[:, :128] + u1[:, 128:]
        vb = jnp.where(low, u0[:, 128:], u1[:, :128])
        vb = vb + pltpu.roll(vb, 64, 1)
        vb0 = jnp.where(low, vb, 0.0)
        vb1 = jnp.where(low, 0.0, vb)

        def two(v):
            hi = v.astype(BF)
            return hi, (v - hi.astype(F32)).astype(BF)
        ah, al = two(va)
        b0h, b0l = two(vb0)
        b1h, b1l = two(vb1)
        w0 = jnp.concatenate([jnp.concatenate([ah, b0h], 1), jnp.concatenate([al, b0l], 1)], 0)
        w1 = jnp.concatenate([jnp.concatenate([b1h, ah], 1), jnp.concatenate([b1l, al], 1)], 0)
        dims = (((1,), (1,)), ((), ()))
        lines = []
        for e, (rows, ww) in enumerate(((one[:, :256], w0), (one[:, 128:], w1))):
            se = lax.dot_general(rows, ww, dims, preferred_element_type=F32)
            se = (se[:, :128] + se[:, 128:]).reshape(16, 16, 128)
            got = jnp.where(gmask[0:1, :] > 0.5, se[0], 0.0)
            for g in range(1, 16):
                got = jnp.where(gmask[g:g + 1, :] > 0.5, se[g], got)
            lines.append(got * scale)
        return jnp.concatenate(lines, 1).astype(BF)

    def q_copy(r, dx):
        tx = lax.rem(x + dx, NX)
        return pltpu.make_async_remote_copy(
            src_ref=sq.at[r, tx], dst_ref=lhs.at[r, x], send_sem=qsem_s.at[r, dx], recv_sem=qsem_r.at[r, dx],
            device_id=(b, tx), device_id_type=MESH)

    def p_copy(r, dx):
        tx = lax.rem(x + dx, NX)
        return pltpu.make_async_remote_copy(
            src_ref=part.at[r, dx - 1], dst_ref=partin.at[r, dx - 1],
            send_sem=psem_s.at[r, dx - 1], recv_sem=psem_r.at[r, dx - 1],
            device_id=(b, tx), device_id_type=MESH)

    def t_copy(r, dx):
        tx = lax.rem(x + dx, NX)
        return pltpu.make_async_remote_copy(
            src_ref=stats.at[r], dst_ref=statin.at[r, dx - 1],
            send_sem=tsem_s.at[r, dx - 1], recv_sem=tsem_r.at[r, dx - 1],
            device_id=(b, tx), device_id_type=MESH)

    @pl.loop(0, NR)
    def _(r):
        mine(r).wait()
        pltpu.make_async_remote_copy(
            src_ref=recv.at[r, pl.ds(0, SRC - 1)], dst_ref=recv.at[r, pl.ds(0, SRC - 1)],
            send_sem=ssem, recv_sem=rsem.at[r],
            device_id=(b, lax.rem(x + 1, NX)), device_id_type=MESH).wait_recv()

        @pl.loop(0, SRC // 16)
        def _(i):
            block = recv[r, pl.ds(i * 16, 16)].astype(F32).reshape(16 * SPR, LANES)
            for q in range(3):
                rf[q, pl.ds(pl.multiple_of(i * 16 * SPR, 16 * SPR), 16 * SPR), :] = block[:, q * 128:(q + 1) * 128]

        @pl.loop(0, SPR // 2)
        def _(h):
            first = gram(2 * h)
            second = gram(2 * h + 1)
            cs[pl.ds(pl.multiple_of(h * 32, 32), 32), :] = jnp.concatenate([first, second], 0)

        turned = jnp.dot(cs[...], perm[...], preferred_element_type=F32)
        cf[0] = turned[:, :128]
        cf[1] = turned[:, 128:]
        for h in range(2):
            by_row = [cf[h, pl.ds(j, SPR, stride=16), :] for j in range(16)]
            for half in range(2):
                cut = [v[:, half * 64:half * 64 + 64] for v in by_row]
                for jj in range(4):
                    sq[r, h * 2 + half, jj] = jnp.concatenate(cut[4 * jj:4 * jj + 4], 1).astype(BF)

        for dx in range(1, NX):
            q_copy(r, dx).start()
        lhs[r, x] = sq[r, x]
        for dx in range(1, NX):
            q_copy(r, dx).wait()

        for dx in (2, 1, 3, 0):
            tx = lax.rem(x + dx, NX)

            @pl.loop(0, 4)
            def _(n):
                cols = pl.ds(pl.multiple_of(tx * 1024 + n * 256, 256), 256)
                acc = jnp.zeros((WID, 256), F32)
                for jj in range(4):
                    acc = acc + jnp.dot(lhs[r, :, jj].reshape(WID, 256), w[jj, :, cols], preferred_element_type=F32)
                here = pl.ds(pl.multiple_of(n * 256, 256), 256)
                if dx == 0:
                    own[:, here] = acc + bias[:, cols]
                else:
                    part[r, dx - 1, :, here] = acc.astype(BF)
            if dx != 0:
                p_copy(r, dx).start()
        for dx in range(1, NX):
            p_copy(r, dx).wait()
        hidden = own[...]
        for dx in range(1, NX):
            hidden = hidden + partin[r, dx - 1].astype(F32)
        own[...] = hidden
        rsum = jnp.sum(hidden, axis=1, keepdims=True)
        rsq = jnp.sum(hidden * hidden, axis=1, keepdims=True)
        at = lane[:WID]
        both = jnp.where(at == 0, rsum, jnp.where(at == 1, rsq, 0.0))
        stats[r] = jnp.concatenate([both, jnp.zeros((128 - WID, 128), F32)], 0).T[:8]
        for dx in range(1, NX):
            t_copy(r, dx).start()
        for dx in range(1, NX):
            t_copy(r, dx).wait()
        total = (stats[r] + statin[r, 0] + statin[r, 1] + statin[r, 2]) * (1.0 / 4096.0)
        mean = total[0:1]
        inv = lax.rsqrt(total[1:2] - mean * mean + 1e-05)
        back = jnp.concatenate([mean, inv, jnp.zeros((126, 128), F32)], 0).T[:WID]
        v = (own[...] - back[:, 0:1]) * back[:, 1:2] * gain[...]
        out[pl.ds(pl.multiple_of(r * WID, WID), WID), :] = (v / (1.0 + jnp.exp(-v))).astype(BF)

    sent = recv.at[:, pl.ds(0, SRC - 1)]
    pltpu.make_async_remote_copy(
        src_ref=sent, dst_ref=sent, send_sem=ssem, recv_sem=rsem.at[0],
        device_id=(b, lax.rem(x + 1, NX)), device_id_type=MESH).wait_send()


def body(tables, bag_ids, bag_lengths, pair_groups, compress, w_hidden, hidden_bias, norm_gain):
    vm = pl.BlockSpec(memory_space=pltpu.VMEM)
    sem = pltpu.SemaphoreType.DMA
    return pl.pallas_call(
        kernel,
        out_shape=jax.ShapeDtypeStruct((128, 1024), BF),
        in_specs=[vm, vm, vm, pl.BlockSpec(memory_space=pltpu.SMEM), vm, pl.BlockSpec(memory_space=pl.ANY), vm, vm],
        out_specs=vm,
        scratch_shapes=[
            pltpu.VMEM((2, ROWS, CH), BF),
            pltpu.VMEM((NR, 32, 2, NX, SPR, LANES), BF),
            pltpu.VMEM((NR, SRC, SPR, LANES), BF),
            pltpu.VMEM((3, SRC * SPR, 128), F32),
            pltpu.VMEM((2, 32, 256), BF),
            pltpu.VMEM((16, 128), F32),
            pltpu.VMEM((4, 2, 32, 256), BF),
            pltpu.VMEM((256, 256), BF),
            pltpu.VMEM((SPR * 16, 256), BF),
            pltpu.VMEM((2, SPR * 16, 128), F32),
            pltpu.VMEM((NR, 4, 4, SPR, 256), BF),
            pltpu.VMEM((NR, 4, 4, SPR, 256), BF),
            pltpu.VMEM((4, 256, 4096), BF),
            pltpu.VMEM((NR, 3, WID, 1024), BF),
            pltpu.VMEM((NR, 3, WID, 1024), BF),
            pltpu.VMEM((WID, 1024), F32),
            pltpu.VMEM((NR, 8, 128), F32),
            pltpu.VMEM((NR, 3, 8, 128), F32),
            sem, sem((NR,)), sem((NR,)), sem((4,)), sem((4,)), sem((NR, 4)), sem((NR, 4)),
            sem((NR, 3)), sem((NR, 3)), sem((NR, 3)), sem((NR, 3)), sem,
        ],
        compiler_params=pltpu.CompilerParams(
            collective_id=0, has_side_effects=True, vmem_limit_bytes=60 << 20),
    )(tables[0].swapaxes(1, 2), bag_ids[0], bag_lengths[0], pair_groups.T,
      compress.swapaxes(1, 2).reshape(32, 32),
      w_hidden.reshape(4, 256, 4096), hidden_bias.reshape(1, 4096), norm_gain.reshape(1, 1024))


def solution(mesh):
    in_specs = (
        P("feat", "batch", None, None),
        P("feat", "batch", None, None),
        P("feat", "batch", None),
        P(),
        P("feat", None, None),
        P("feat", None, None, None),
        P(),
        P("feat"),
    )
    out_specs = P("batch", "feat")
    return jax.shard_map(body, mesh=mesh, in_specs=in_specs, out_specs=out_specs, check_vma=False)
```

```python
import jax
import jax.numpy as jnp
from jax import lax
from jax.experimental import pallas as pl
from jax.experimental.pallas import tpu as pltpu
from jax.sharding import PartitionSpec as P

MESH = pl.DeviceIdType.MESH
BF = jnp.bfloat16
F32 = jnp.float32
NY, NZ, NX = 4, 8, 4
SRC = 256
SD = 32
DIM = 192
ROWS = 2048
LANES = 2 * DIM
CH = 256
NR = 4
SPR = SD // NR
WID = 4 * SPR
UNITS = 32
UPR = UNITS // NR
LAG = 3


def kernel(tt_hbm, ids_hbm, lens_hbm, pairs, comp, w_hbm, bias, gain, out,
           tt, ids, lens, oh, send, recv, rf, cpart, gmask, cexp, perm, cs, cf, sq, lhs, w, part, partin, own, stats, statin,
           ssem, rsem, lsem, csem_s, csem_r, qsem_s, qsem_r, psem_s, psem_r, tsem_s, tsem_r, wsem, isem):
    b = lax.axis_index("batch")
    x = lax.axis_index("feat")
    y = b // 16
    z = lax.rem(b // 2, NZ)
    c = lax.rem(b, 2)
    me = x * 64 + b

    bar = pltpu.get_barrier_semaphore()

    along_z = [lax.rem(z + k, NZ) * 2 for k in range(NZ)]
    for dx in (2, 1, 3, 0):
        tx = lax.rem(x + dx, NX)
        for dy in (2, 1, 3, 0):
            plane = lax.rem(y + dy, NY) * (2 * NZ)
            for k in (4, 3, 5, 2, 6, 1, 7, 0):
                if dx + dy + k > 0:
                    pl.semaphore_signal(bar, inc=1, device_id=(plane + along_z[k] + c, tx), device_id_type=MESH)
                pl.semaphore_signal(bar, inc=1, device_id=(plane + along_z[k] + 1 - c, tx), device_id_type=MESH)

    loads = [pltpu.make_async_copy(tt_hbm, tt, isem.at[0]), pltpu.make_async_copy(ids_hbm, ids, isem.at[1]),
             pltpu.make_async_copy(lens_hbm, lens, isem.at[2])]
    for load in loads:
        load.start()

    @pl.loop(0, 16)
    def _(j):
        for p in range(4):
            pltpu.make_async_copy(
                w_hbm.at[p, pl.ds(pl.multiple_of(j * 16, 16), 16)],
                w.at[j // 4, pl.ds(pl.multiple_of(lax.rem(j, 4) * 64 + p * 16, 16), 16)], wsem).start()

    row = lax.broadcasted_iota(jnp.int32, (256, 256), 0)
    col = lax.broadcasted_iota(jnp.int32, (256, 256), 1)
    perm[...] = (col == lax.rem(row // 8, 16) * 16 + row // 128 * 8 + lax.rem(row, 8)).astype(F32).astype(BF)
    lane_pair = lax.broadcasted_iota(jnp.int32, (16, 128), 1) // 8
    first = jnp.zeros((16, 128), jnp.int32)
    for p in range(16):
        first = jnp.where(lane_pair == p, pairs[0, p], first)
    gmask[...] = (first == lax.broadcasted_iota(jnp.int32, (16, 128), 0)).astype(F32)
    row_pair = lax.broadcasted_iota(jnp.int32, (32, 256), 0) // 8
    second = jnp.zeros((32, 256), jnp.int32)
    for p in range(4):
        second = jnp.where(row_pair == p, pairs[1, x * 4 + p], second)
    hit = second == lax.broadcasted_iota(jnp.int32, (32, 256), 1) // 16
    slot = lax.broadcasted_iota(jnp.int32, (32, 256), 0)
    member = lax.rem(lax.broadcasted_iota(jnp.int32, (32, 256), 1), 16)
    for e in range(2):
        spread = (slot == 2 * member + e).astype(F32).astype(BF)
        cpart[e] = jnp.where(hit, jnp.dot(comp[...], spread, preferred_element_type=F32), 0.0).astype(BF)

    quarter = lax.broadcasted_iota(jnp.int32, (1, 128), 1) // WID

    for load in loads:
        load.wait()

    def where_to(u, q):
        t = u * NR + q
        cy = lax.rem(y + q + t // 8, NY)
        cz = lax.rem(z + lax.rem(3 * lax.rem(t, 8) + 4, 8), NZ)
        return cy * NZ + cz

    def pool(r, u):
        chips = [where_to(u, q) for q in range(NR)]

        def lanes_of(ref):
            tiles = []
            for h in range(2):
                made = None
                for m in range(NR):
                    k = h * NR + m
                    at = pl.multiple_of((chips[k // 2] * 2 + k % 2) * 128, 128)
                    piece = pltpu.roll(ref[:, pl.ds(at, 128)], lax.rem(m * WID - r * WID + 128, 128), 1)
                    made = piece if m == 0 else jnp.where(quarter == m, piece, made)
                tiles.append(made)
            return jnp.concatenate(tiles, axis=1)

        both_lengths = lanes_of(lens)
        sums = []
        for e in range(2):
            length = both_lengths[e:e + 1]
            four = lanes_of(ids.at[e])
            live = [jnp.where(length > k, four[k:k + 1], -4096 - k) for k in range(4)]
            keyed, counts = [], []
            for k in range(4):
                count = jnp.ones((1, CH), F32)
                for m in range(k + 1, 4):
                    count = count + jnp.where(live[m] == live[k], 1.0, 0.0)
                key = live[k]
                for m in range(k):
                    key = jnp.where(live[m] == live[k], -4096, key)
                keyed.append(key)
                counts.append(count.astype(BF))
            base = lax.broadcasted_iota(jnp.int32, (256, CH), 0).astype(F32).astype(BF)
            for j in range(8):
                hot = jnp.zeros((256, CH), BF)
                for k in range(3, -1, -1):
                    key = (keyed[k] - 256 * j).astype(F32).astype(BF)
                    hot = jnp.where(base == key, counts[k], hot)
                oh[e, pl.ds(j * 256, 256), :] = hot
            sums.append(jnp.dot(tt[e], oh[e], preferred_element_type=F32))
        full = jnp.concatenate([sums[0], sums[1][128:], sums[1][:128]], axis=0)
        made = full.T.reshape(NR, 2, NX, SPR, LANES).astype(BF)
        for q in range(NR):
            send[r, chips[q]] = made[q]

    def send_one(r, u, q, dx, dc):
        chip = where_to(u, q)
        tx = lax.rem(x + dx, NX)
        tc = lax.rem(c + dc, 2)
        pltpu.make_async_remote_copy(
            src_ref=send.at[r, chip, tc, tx], dst_ref=recv.at[r, me], send_sem=ssem, recv_sem=rsem.at[r],
            device_id=(chip * 2 + tc, tx), device_id_type=MESH).start()

    def send_unit(t):
        r = t // UPR
        u = lax.rem(t, UPR)
        for shift in range(NX):
            for dc in range(2):
                for q in range(NR):
                    dx = (shift + q) % NX
                    if dx == 0 and dc == 0 and q == 4 % NR:
                        @pl.when(u != 4 // NR)
                        def _():
                            send_one(r, u, q, dx, dc)
                    else:
                        send_one(r, u, q, dx, dc)

    def c_copy(dx):
        tx = lax.rem(x + dx, NX)
        return pltpu.make_async_remote_copy(
            src_ref=cpart, dst_ref=cexp.at[x], send_sem=csem_s.at[dx], recv_sem=csem_r.at[dx],
            device_id=(b, tx), device_id_type=MESH)

    @pl.loop(0, UNITS)
    def _(t):
        pool(t // UPR, lax.rem(t, UPR))

        @pl.when(t == LAG)
        def _():
            pl.semaphore_wait(bar, 255)
            for dx in range(1, NX):
                c_copy(dx).start()

            @pl.loop(0, LAG - 1)
            def _(u):
                send_unit(u)

        @pl.when(t >= LAG)
        def _():
            send_unit(t - 1)

    send_unit(UNITS - 1)

    def mine(r):
        return pltpu.make_async_copy(send.at[r, y * NZ + z, c, x], recv.at[r, me], lsem.at[r])

    for r in range(NR):
        mine(r).start()
    cexp[x] = cpart[...]
    for dx in range(1, NX):
        c_copy(dx).wait()
    pltpu.make_async_copy(w_hbm, w, wsem).wait()

    lane = lax.broadcasted_iota(jnp.int32, (128, 128), 1)
    scale = float(DIM) ** -0.5
    low = lane < 64

    def gram(s):
        one = jnp.concatenate([rf[q, pl.ds(s, SRC, stride=SPR), :] for q in range(3)], 1).astype(BF)
        u0 = jnp.dot(cexp[:, 0].reshape(128, 256), one[:, :256], preferred_element_type=F32)
        u1 = jnp.dot(cexp[:, 1].reshape(128, 256), one[:, 128:], preferred_element_type=F32)
        va = u0[:, :128] + u1[:, 128:]
        vb = jnp.where(low, u0[:, 128:], u1[:, :128])
        vb = vb + pltpu.roll(vb, 64, 1)
        vb0 = jnp.where(low, vb, 0.0)
        vb1 = jnp.where(low, 0.0, vb)

        def two(v):
            hi = v.astype(BF)
            return hi, (v - hi.astype(F32)).astype(BF)
        ah, al = two(va)
        b0h, b0l = two(vb0)
        b1h, b1l = two(vb1)
        w0 = jnp.concatenate([jnp.concatenate([ah, b0h], 1), jnp.concatenate([al, b0l], 1)], 0)
        w1 = jnp.concatenate([jnp.concatenate([b1h, ah], 1), jnp.concatenate([b1l, al], 1)], 0)
        dims = (((1,), (1,)), ((), ()))
        lines = []
        for e, (rows, ww) in enumerate(((one[:, :256], w0), (one[:, 128:], w1))):
            se = lax.dot_general(rows, ww, dims, preferred_element_type=F32)
            se = (se[:, :128] + se[:, 128:]).reshape(16, 16, 128)
            got = jnp.where(gmask[0:1, :] > 0.5, se[0], 0.0)
            for g in range(1, 16):
                got = jnp.where(gmask[g:g + 1, :] > 0.5, se[g], got)
            lines.append(got * scale)
        return jnp.concatenate(lines, 1).astype(BF)

    def q_copy(r, dx):
        tx = lax.rem(x + dx, NX)
        return pltpu.make_async_remote_copy(
            src_ref=sq.at[r, tx], dst_ref=lhs.at[r, x], send_sem=qsem_s.at[r, dx], recv_sem=qsem_r.at[r, dx],
            device_id=(b, tx), device_id_type=MESH)

    def p_copy(r, dx):
        tx = lax.rem(x + dx, NX)
        return pltpu.make_async_remote_copy(
            src_ref=part.at[r, dx - 1], dst_ref=partin.at[r, dx - 1],
            send_sem=psem_s.at[r, dx - 1], recv_sem=psem_r.at[r, dx - 1],
            device_id=(b, tx), device_id_type=MESH)

    def t_copy(r, dx):
        tx = lax.rem(x + dx, NX)
        return pltpu.make_async_remote_copy(
            src_ref=stats.at[r], dst_ref=statin.at[r, dx - 1],
            send_sem=tsem_s.at[r, dx - 1], recv_sem=tsem_r.at[r, dx - 1],
            device_id=(b, tx), device_id_type=MESH)

    @pl.loop(0, NR)
    def _(r):
        mine(r).wait()
        pltpu.make_async_remote_copy(
            src_ref=recv.at[r, pl.ds(0, SRC - 1)], dst_ref=recv.at[r, pl.ds(0, SRC - 1)],
            send_sem=ssem, recv_sem=rsem.at[r],
            device_id=(b, lax.rem(x + 1, NX)), device_id_type=MESH).wait_recv()

        @pl.loop(0, SRC // 16)
        def _(i):
            block = recv[r, pl.ds(i * 16, 16)].astype(F32).reshape(16 * SPR, LANES)
            for q in range(3):
                rf[q, pl.ds(pl.multiple_of(i * 16 * SPR, 16 * SPR), 16 * SPR), :] = block[:, q * 128:(q + 1) * 128]

        @pl.loop(0, SPR // 2)
        def _(h):
            first = gram(2 * h)
            second = gram(2 * h + 1)
            cs[pl.ds(pl.multiple_of(h * 32, 32), 32), :] = jnp.concatenate([first, second], 0)

        turned = jnp.dot(cs[...], perm[...], preferred_element_type=F32)
        cf[0] = turned[:, :128]
        cf[1] = turned[:, 128:]
        for h in range(2):
            by_row = [cf[h, pl.ds(j, SPR, stride=16), :] for j in range(16)]
            for half in range(2):
                cut = [v[:, half * 64:half * 64 + 64] for v in by_row]
                for jj in range(4):
                    sq[r, h * 2 + half, jj] = jnp.concatenate(cut[4 * jj:4 * jj + 4], 1).astype(BF)

        for dx in range(1, NX):
            q_copy(r, dx).start()
        lhs[r, x] = sq[r, x]
        for dx in range(1, NX):
            q_copy(r, dx).wait()

        for dx in (2, 1, 3, 0):
            tx = lax.rem(x + dx, NX)

            @pl.loop(0, 4)
            def _(n):
                cols = pl.ds(pl.multiple_of(tx * 1024 + n * 256, 256), 256)
                acc = jnp.zeros((WID, 256), F32)
                for jj in range(4):
                    acc = acc + jnp.dot(lhs[r, :, jj].reshape(WID, 256), w[jj, :, cols], preferred_element_type=F32)
                here = pl.ds(pl.multiple_of(n * 256, 256), 256)
                if dx == 0:
                    own[:, here] = acc + bias[:, cols]
                else:
                    part[r, dx - 1, :, here] = acc.astype(BF)
            if dx != 0:
                p_copy(r, dx).start()
        for dx in range(1, NX):
            p_copy(r, dx).wait()
        hidden = own[...]
        for dx in range(1, NX):
            hidden = hidden + partin[r, dx - 1].astype(F32)
        own[...] = hidden
        rsum = jnp.sum(hidden, axis=1, keepdims=True)
        rsq = jnp.sum(hidden * hidden, axis=1, keepdims=True)
        at = lane[:WID]
        both = jnp.where(at == 0, rsum, jnp.where(at == 1, rsq, 0.0))
        stats[r] = jnp.concatenate([both, jnp.zeros((128 - WID, 128), F32)], 0).T[:8]
        for dx in range(1, NX):
            t_copy(r, dx).start()
        for dx in range(1, NX):
            t_copy(r, dx).wait()
        total = (stats[r] + statin[r, 0] + statin[r, 1] + statin[r, 2]) * (1.0 / 4096.0)
        mean = total[0:1]
        inv = lax.rsqrt(total[1:2] - mean * mean + 1e-05)
        back = jnp.concatenate([mean, inv, jnp.zeros((126, 128), F32)], 0).T[:WID]
        v = (own[...] - back[:, 0:1]) * back[:, 1:2] * gain[...]
        out[pl.ds(pl.multiple_of(r * WID, WID), WID), :] = (v / (1.0 + jnp.exp(-v))).astype(BF)

    sent = recv.at[:, pl.ds(0, SRC - 1)]
    pltpu.make_async_remote_copy(
        src_ref=sent, dst_ref=sent, send_sem=ssem, recv_sem=rsem.at[0],
        device_id=(b, lax.rem(x + 1, NX)), device_id_type=MESH).wait_send()


def body(tables, bag_ids, bag_lengths, pair_groups, compress, w_hidden, hidden_bias, norm_gain):
    vm = pl.BlockSpec(memory_space=pltpu.VMEM)
    far = pl.BlockSpec(memory_space=pl.ANY)
    sem = pltpu.SemaphoreType.DMA
    return pl.pallas_call(
        kernel,
        out_shape=jax.ShapeDtypeStruct((128, 1024), BF),
        in_specs=[far, far, far, pl.BlockSpec(memory_space=pltpu.SMEM), vm, far, vm, vm],
        out_specs=vm,
        scratch_shapes=[
            pltpu.VMEM((2, DIM, ROWS), BF),
            pltpu.VMEM((2, 4, 8192), jnp.int32),
            pltpu.VMEM((2, 8192), jnp.int32),
            pltpu.VMEM((2, ROWS, CH), BF),
            pltpu.VMEM((NR, 32, 2, NX, SPR, LANES), BF),
            pltpu.VMEM((NR, SRC, SPR, LANES), BF),
            pltpu.VMEM((3, SRC * SPR, 128), F32),
            pltpu.VMEM((2, 32, 256), BF),
            pltpu.VMEM((16, 128), F32),
            pltpu.VMEM((4, 2, 32, 256), BF),
            pltpu.VMEM((256, 256), BF),
            pltpu.VMEM((SPR * 16, 256), BF),
            pltpu.VMEM((2, SPR * 16, 128), F32),
            pltpu.VMEM((NR, 4, 4, SPR, 256), BF),
            pltpu.VMEM((NR, 4, 4, SPR, 256), BF),
            pltpu.VMEM((4, 256, 4096), BF),
            pltpu.VMEM((NR, 3, WID, 1024), BF),
            pltpu.VMEM((NR, 3, WID, 1024), BF),
            pltpu.VMEM((WID, 1024), F32),
            pltpu.VMEM((NR, 8, 128), F32),
            pltpu.VMEM((NR, 3, 8, 128), F32),
            sem, sem((NR,)), sem((NR,)), sem((4,)), sem((4,)), sem((NR, 4)), sem((NR, 4)),
            sem((NR, 3)), sem((NR, 3)), sem((NR, 3)), sem((NR, 3)), sem, sem((3,)),
        ],
        compiler_params=pltpu.CompilerParams(
            collective_id=0, has_side_effects=True, vmem_limit_bytes=60 << 20),
    )(tables[0].swapaxes(1, 2), bag_ids[0], bag_lengths[0], pair_groups.T,
      compress.swapaxes(1, 2).reshape(32, 32),
      w_hidden.reshape(4, 256, 4096), hidden_bias.reshape(1, 4096), norm_gain.reshape(1, 1024))


def solution(mesh):
    in_specs = (
        P("feat", "batch", None, None),
        P("feat", "batch", None, None),
        P("feat", "batch", None),
        P(),
        P("feat", None, None),
        P("feat", None, None, None),
        P(),
        P("feat"),
    )
    out_specs = P("batch", "feat")
    return jax.shard_map(body, mesh=mesh, in_specs=in_specs, out_specs=out_specs, check_vma=False)
```
